32 devices in a mesh: grp: 4 (over y, x), lane: 8 (over z, core).
Axes of the slice: x: 2, y: 2, z: 4, core: 2. Of those that a mesh axis runs over, the one named last changes fastest.
Arguments:
- ctrl_factor: bfloat16 [49152, 512], P(('grp', 'lane')), may hold values from -6 to 6
- obs_factor: bfloat16 [49152, 512], P(('grp', 'lane')), may hold values from -6 to 6
- block_cols: int32 [384, 4], P(('grp', 'lane')), may hold values from -1 to 383, as said below
- mass_blocks: bfloat16 [384, 4, 128, 128], P(('grp', 'lane')), may hold values from -0.25 to 0.25
Outputs:
- cross_gram: float32 [512, 512], P('lane')
The draws below stay inside these ranges and needn't reach their ends.
Inputs may be any that keep to these rules, and one draw needn't show every extreme that they name: block_cols[g, 0] is g; every other entry is -1 or a block index within 2 of g, distinct within a row; row block 0 has an empty slot.
All inputs are finite; a program needn't handle non-finite values.
Results may differ from the reference program's by a relative error of at most 0.0029.
Values may be sent and summed in bfloat16 or wider, within the bound.
A program may use at most 64 MiB of HBM per device.

```python
import jax
import jax.numpy as jnp
from jax import lax

R = 512
BS = 128
S = 4
NB = 384
N = 49152


def draw_block_cols(key, part):
    rowids = jnp.arange(NB, dtype=jnp.int32)
    keys = jax.random.split(jax.random.fold_in(key, 7), NB)
    offsets = jnp.array([-2, -1, 1, 2], dtype=jnp.int32)
    shuffled = jax.vmap(lambda k: jax.random.permutation(k, offsets))(keys)[:, :S - 1]
    cols = jnp.concatenate([rowids[:, None], rowids[:, None] + shuffled], axis=1)
    live_count = jax.random.randint(jax.random.fold_in(key, 11), (NB,), 1, S + 1)
    slots = jnp.arange(S, dtype=jnp.int32)
    valid = (slots[None, :] < live_count[:, None]) & (cols >= 0) & (cols < NB)
    return jnp.where(valid, cols, -1).astype(jnp.int32)


def raised(values, stream_key, source, target, blocks, factor):
    owner, partner = [(jnp.arange(values.shape[dim]) // (values.shape[dim] // blocks)).reshape([-1 if axis == dim else 1 for axis in range(values.ndim)]) for dim in (source, target)]
    chosen = jax.random.permutation(stream_key, blocks)[partner]
    strong = (owner == chosen) | (owner == (partner + blocks // 2) % blocks)
    return jnp.where(strong, factor * values, values)


def levels(own_key, dims, shards, smallest, largest):
    loudness, own = 1.0, jax.random.fold_in(own_key, 6)
    for dim, shards_of in shards:
        draws = jnp.exp(jax.random.uniform(jax.random.fold_in(own, dim), (shards_of,), jnp.float32, smallest / len(shards), largest / len(shards)))
        loudness = loudness * jnp.repeat(draws, dims[dim] // shards_of).reshape([-1 if axis == dim else 1 for axis in range(len(dims))])
    return loudness


def bell_draw(key, shape, deviation, limit, pieces=(), kind=jnp.bfloat16):
    drawn = jax.random.normal(key, shape, jnp.float32) * deviation
    if len(pieces) > 0:
        drawn = levels(key, shape, pieces, -0.22, 0.18) * drawn
    return jnp.clip(drawn, min=-limit, max=limit).astype(kind)


def heavy_noise(rng, dims, width, limit, cuts, heavy, held_as=jnp.bfloat16):
    drawn = width * jax.random.normal(rng, dims, jnp.float32)
    if cuts:
        drawn = drawn * levels(rng, dims, cuts, -0.22, 0.18)
    return jnp.clip(raised(drawn, jax.random.fold_in(rng, 3), *heavy), -limit, limit).astype(held_as)


def setup_inputs(seed: int = 0) -> dict:
    key_list = jax.random.split(jax.random.key(seed), 5)
    return {
        "ctrl_factor": bell_draw(key_list[0], (N, R), 1.0, 6.0, ((0, 32),)),
        "obs_factor": heavy_noise(key_list[1], (N, R), 1.0, 6.0, ((0, 32),), (0, 1, 32, 2.75)),
        "block_cols": draw_block_cols(jax.random.fold_in(key_list[4], 71), 0),
        "mass_blocks": bell_draw(key_list[3], (NB, S, BS, BS), (S * BS) ** -0.5, 0.25, ((0, 32),)),
    }


def reference(ctrl_factor, obs_factor, block_cols, mass_blocks):
    nblk = block_cols.shape[0]
    blocks_ctrl = ctrl_factor.reshape(nblk, BS, R)

    def one_row(args):
        cols, blocks = args
        live = (cols >= 0).astype(jnp.float32)
        safe = jnp.clip(cols, 0, nblk - 1).astype(jnp.int32)
        picked = blocks_ctrl[safe].astype(jnp.float32)
        masked = blocks.astype(jnp.float32) * live[:, None, None]
        return jnp.einsum("sij,sjr->ir", masked, picked).astype(jnp.bfloat16)

    mass_ctrl = lax.map(one_row, (block_cols, mass_blocks)).reshape(nblk * BS, R)
    return lax.dot_general(obs_factor, mass_ctrl, (((0,), (0,)), ((), ())), preferred_element_type=jnp.float32)
```

```python
import functools

import jax
import jax.numpy as jnp
from jax import lax
from jax.experimental import pallas as pl
from jax.experimental.pallas import tpu as pltpu
from jax.sharding import PartitionSpec as P

MESH = pl.DeviceIdType.MESH
F32 = jnp.float32
BF16 = jnp.bfloat16
CORES = 2
CHUNKS = 4


def row_order(width, lanes, fused):
    if not fused:
        return [(0, 0, width)]
    zs = lanes // CORES
    piece = width // lanes
    return [
        ((z * CORES + core) * piece, (core * zs + z) * piece, piece)
        for core in range(CORES)
        for z in range(zs)
    ]


def kernel(
    groups, lanes, fused, nblk, bs, cols_hbm, ctrl_hbm, obs_hbm, mass_hbm, out_ref,
    cols_ref, ctrl_v, obs_v, mass_v, band, obs_in, obs_edge, mc_in, mc_edge, gram,
    send_a, recv_a, send_z, recv_z, gath,
    load_sem, hs_sem, hr_sem, as_sem, ar_sem, zs_sem, zr_sem, gs_sem, gr_sem,
):
    q = lax.axis_index("grp")
    lane = lax.axis_index("lane")
    zs = lanes // CORES
    core = lax.rem(lane, CORES)
    z = lane // CORES
    me = q * lanes + lane
    last = groups * lanes - 1
    rows = nblk * bs
    halo = 2 * bs
    width = ctrl_v.shape[1]

    loads = [
        pltpu.make_async_copy(ctrl_hbm, ctrl_v.at[pl.ds(halo, rows)], load_sem.at[0]),
        pltpu.make_async_copy(mass_hbm, mass_v, load_sem.at[1]),
        pltpu.make_async_copy(obs_hbm, obs_v, load_sem.at[2]),
        pltpu.make_async_copy(cols_hbm, cols_ref, load_sem.at[3]),
    ]
    def place(index):
        return (index // lanes, lax.rem(index, lanes))

    def grp_peer(k):
        return (lax.rem(q + k, groups), lane)

    def turn(i):
        return i + (1 - lax.rem(q, 2)) * (groups - 2 * i)

    def z_peer(k):
        return (q, lax.rem(z + k, zs) * CORES + core)

    partner = (q, lane + 1 - 2 * core)
    barrier = pltpu.get_barrier_semaphore()

    @pl.when(me > 0)
    def _():
        pl.semaphore_signal(barrier, inc=1, device_id=place(me - 1), device_id_type=MESH)

    @pl.when(me < last)
    def _():
        pl.semaphore_signal(barrier, inc=1, device_id=place(me + 1), device_id_type=MESH)

    peers = 0
    if fused:
        pl.semaphore_signal(barrier, inc=1, device_id=partner, device_id_type=MESH)
        for k in range(1, groups):
            pl.semaphore_signal(barrier, inc=1, device_id=grp_peer(k), device_id_type=MESH)
        for k in range(1, zs):
            pl.semaphore_signal(barrier, inc=1, device_id=z_peer(k), device_id_type=MESH)
        peers = groups + zs - 1

    for load in loads:
        load.start()

    @pl.when((me > 0) & (me < last))
    def _():
        pl.semaphore_wait(barrier, peers + 2)

    @pl.when((me == 0) | (me == last))
    def _():
        pl.semaphore_wait(barrier, peers + 1)

    chunk = width // CHUNKS
    chunks = [slice(h * chunk, (h + 1) * chunk) for h in range(CHUNKS)]

    def to_left(h):
        return pltpu.make_async_remote_copy(
            src_ref=ctrl_v.at[pl.ds(halo, halo), chunks[h]],
            dst_ref=ctrl_v.at[pl.ds(halo + rows, halo), chunks[h]],
            send_sem=hs_sem.at[0, h],
            recv_sem=hr_sem.at[1, h],
            device_id=place(me - 1),
            device_id_type=MESH,
        )

    def to_right(h):
        return pltpu.make_async_remote_copy(
            src_ref=ctrl_v.at[pl.ds(rows, halo), chunks[h]],
            dst_ref=ctrl_v.at[pl.ds(0, halo), chunks[h]],
            send_sem=hs_sem.at[1, h],
            recv_sem=hr_sem.at[0, h],
            device_id=place(me + 1),
            device_id_type=MESH,
        )

    loads[0].wait()

    for h in range(CHUNKS):
        @pl.when(me > 0)
        def _():
            to_left(h).start()

        @pl.when(me < last)
        def _():
            to_right(h).start()

    @pl.when(me == 0)
    def _():
        ctrl_v[pl.ds(0, halo), :] = jnp.zeros((halo, width), BF16)

    @pl.when(me == last)
    def _():
        ctrl_v[pl.ds(halo + rows, halo), :] = jnp.zeros((halo, width), BF16)

    pairs = nblk // 2
    zero = jnp.zeros((bs, bs), BF16)
    slots = mass_v.shape[1]

    def build(p):
        for j in range(2):
            g = 2 * p + j
            offsets = []
            for s in range(1, slots):
                col = cols_ref[s, g]
                offsets.append(jnp.where(col >= 0, col - (me * nblk + g), 99))
            for b in range(6):
                d = b - 2 - j
                if d == 0:
                    block = mass_v[g, 0]
                elif abs(d) > 2:
                    block = zero
                else:
                    block = zero
                    for s in range(1, slots):
                        block = jnp.where(offsets[s - 1] == d, mass_v[g, s], block)
                band[p, j * bs:(j + 1) * bs, b * bs:(b + 1) * bs] = block

    def product(p, cols):
        return jnp.dot(
            band[p], ctrl_v[pl.ds(p * halo, 3 * halo), cols], preferred_element_type=F32
        ).astype(BF16)

    order = row_order(width, lanes, fused)

    def turned(p, target, at):
        block = obs_v[pl.ds(p * halo, halo), :].T
        for source, dest, count in order:
            target[dest:dest + count, at:at + halo] = block[source:source + count, :]

    loads[1].wait()
    loads[3].wait()
    for p in range(1, pairs - 1):
        build(p)
        mc_in[(p - 1) * halo:p * halo, :] = product(p, slice(0, width))
    build(0)
    build(pairs - 1)
    loads[2].wait()
    for p in range(1, pairs - 1):
        turned(p, obs_in, (p - 1) * halo)
    turned(0, obs_edge, 0)
    turned(pairs - 1, obs_edge, halo)
    half = width // 2
    for r in range(2):
        gram[r * half:(r + 1) * half, :] = jnp.dot(
            obs_in[r * half:(r + 1) * half, :], mc_in[...], preferred_element_type=F32
        )

    def edges(h):
        @pl.when(me > 0)
        def _():
            to_right(h).wait_recv()

        mc_edge[0:halo, chunks[h]] = product(0, chunks[h])

        @pl.when(me < last)
        def _():
            to_left(h).wait_recv()

        mc_edge[halo:2 * halo, chunks[h]] = product(pairs - 1, chunks[h])

    def finished(start, count, cols):
        return gram[pl.ds(start, count), cols] + jnp.dot(
            obs_edge[pl.ds(start, count), :], mc_edge[:, cols], preferred_element_type=F32
        )

    def halo_sent():
        for h in range(CHUNKS):
            @pl.when(me > 0)
            def _():
                to_left(h).wait_send()

            @pl.when(me < last)
            def _():
                to_right(h).wait_send()

    if not fused:
        for h in range(CHUNKS):
            edges(h)
        out_ref[...] = finished(0, width, slice(0, width))
        halo_sent()
        return

    theirs = pl.multiple_of((1 - core) * half, half)
    mine = pl.multiple_of(core * half, half)
    piece = width // lanes

    def copy_a(h):
        return pltpu.make_async_remote_copy(
            src_ref=send_a.at[h], dst_ref=recv_a.at[h],
            send_sem=as_sem.at[h], recv_sem=ar_sem.at[h],
            device_id=partner, device_id_type=MESH,
        )

    def copy_z(h, k):
        return pltpu.make_async_remote_copy(
            src_ref=send_z.at[h, lax.rem(z + k, zs)], dst_ref=recv_z.at[h, k - 1],
            send_sem=zs_sem.at[h, k - 1], recv_sem=zr_sem.at[h, k - 1],
            device_id=z_peer(k), device_id_type=MESH,
        )

    def copy_g(h, k):
        return pltpu.make_async_remote_copy(
            src_ref=gath.at[h, q], dst_ref=gath.at[h, q],
            send_sem=gs_sem.at[h, k - 1], recv_sem=gr_sem.at[h, k - 1],
            device_id=grp_peer(k), device_id_type=MESH,
        )

    def stage_edges(h):
        edges(h)
        send_a[h] = finished(theirs, half, chunks[h])
        copy_a(h).start()
        gram[pl.ds(mine, half), chunks[h]] = finished(mine, half, chunks[h])

    def stage_core(h):
        copy_a(h).wait_recv()
        total = gram[pl.ds(mine, half), chunks[h]] + recv_a[h]
        gram[pl.ds(mine, half), chunks[h]] = total
        send_z[h] = total.astype(BF16).reshape(zs, piece, chunk)
        for k in range(1, zs):
            copy_z(h, k).start()

    def stage_z(h):
        share = gram[pl.ds(pl.multiple_of(core * half + z * piece, piece), piece), chunks[h]]
        for k in range(1, zs):
            copy_z(h, k).wait_recv()
            share = share + recv_z[h, k - 1].astype(F32)
        gath[h, q] = share.astype(BF16)
        for i in range(1, groups):
            copy_g(h, turn(i)).start()

    def stage_grp(h):
        for k in range(1, groups):
            copy_g(h, k).wait_recv()
        total = gath[h, 0].astype(F32)
        for k in range(1, groups):
            total = total + gath[h, k].astype(F32)
        out_ref[:, chunks[h]] = total

    for h in range(CHUNKS):
        stage_edges(h)
        if h >= 1:
            stage_core(h - 1)
    stage_core(CHUNKS - 1)
    for h in range(CHUNKS):
        stage_z(h)
    for h in range(CHUNKS):
        stage_grp(h)
    halo_sent()
    for h in range(CHUNKS):
        copy_a(h).wait_send()
        for k in range(1, zs):
            copy_z(h, k).wait_send()
        for k in range(1, groups):
            copy_g(h, k).wait_send()


def solution(mesh):
    groups, lanes = mesh.shape["grp"], mesh.shape["lane"]

    def shards(ctrl_factor, obs_factor, block_cols, mass_blocks):
        nblk, slots = block_cols.shape
        rows, width = ctrl_factor.shape
        bs = rows // nblk
        halo = 2 * bs
        fused = width % (lanes * groups * 16) == 0
        pairs = nblk // 2
        zs = lanes // CORES
        half, chunk = width // 2, width // CHUNKS
        piece = width // lanes
        out_rows = width // lanes if fused else width
        dma = pltpu.SemaphoreType.DMA
        result = pl.pallas_call(
            functools.partial(kernel, groups, lanes, fused, nblk, bs),
            out_shape=pltpu.VMEM((out_rows, width), F32),
            in_specs=[pl.BlockSpec(memory_space=pltpu.HBM)] * 4,
            out_specs=pl.BlockSpec(memory_space=pltpu.VMEM),
            scratch_shapes=[
                pltpu.SMEM((slots, nblk), jnp.int32),
                pltpu.VMEM((rows + 2 * halo, width), BF16),
                pltpu.VMEM((rows, width), BF16),
                pltpu.VMEM((nblk, slots, bs, bs), BF16),
                pltpu.VMEM((pairs, halo, 3 * halo), BF16),
                pltpu.VMEM((width, rows - 2 * halo), BF16),
                pltpu.VMEM((width, 2 * halo), BF16),
                pltpu.VMEM((rows - 2 * halo, width), BF16),
                pltpu.VMEM((2 * halo, width), BF16),
                pltpu.VMEM((width, width), F32),
                pltpu.VMEM((CHUNKS, half, chunk), F32),
                pltpu.VMEM((CHUNKS, half, chunk), F32),
                pltpu.VMEM((CHUNKS, zs, piece, chunk), BF16),
                pltpu.VMEM((CHUNKS, zs - 1, piece, chunk), BF16),
                pltpu.VMEM((CHUNKS, groups, piece, chunk), BF16),
                dma((4,)), dma((2, CHUNKS)), dma((2, CHUNKS)), dma((CHUNKS,)), dma((CHUNKS,)),
                dma((CHUNKS, zs - 1)), dma((CHUNKS, zs - 1)),
                dma((CHUNKS, groups - 1)), dma((CHUNKS, groups - 1)),
            ],
            compiler_params=pltpu.CompilerParams(
                collective_id=0, has_side_effects=True, vmem_limit_bytes=56 * 2**20
            ),
        )(block_cols.T, ctrl_factor, obs_factor, mass_blocks)
        if fused:
            return result
        share = lax.psum_scatter(result, "lane", scatter_dimension=0, tiled=True)
        return lax.psum(share, "grp")

    placed = (
        P(("grp", "lane"), None),
        P(("grp", "lane"), None),
        P(("grp", "lane"), None),
        P(("grp", "lane"), None, None, None),
    )
    return jax.shard_map(
        shards, mesh=mesh, in_specs=placed, out_specs=P("lane", None), check_vma=False
    )
```

```python
import functools

import jax
import jax.numpy as jnp
from jax import lax
from jax.experimental import pallas as pl
from jax.experimental.pallas import tpu as pltpu
from jax.sharding import PartitionSpec as P

MESH = pl.DeviceIdType.MESH
F32 = jnp.float32
BF16 = jnp.bfloat16
CORES = 2
CHUNKS = 4


def row_order(width, lanes, fused):
    if not fused:
        return [(0, 0, width)]
    zs = lanes // CORES
    piece = width // lanes
    return [
        ((z * CORES + core) * piece, (core * zs + z) * piece, piece)
        for core in range(CORES)
        for z in range(zs)
    ]


def kernel(
    groups, lanes, fused, nblk, bs, cols_hbm, ctrl_hbm, obs_hbm, mass_hbm, out_ref,
    cols_ref, ctrl_v, obs_v, mass_v, band, obs_in, obs_edge, mc_in, mc_local, mc_edge, gram,
    send_a, recv_a, send_z, recv_z, gath,
    load_sem, hs_sem, hr_sem, as_sem, ar_sem, zs_sem, zr_sem, gs_sem, gr_sem, tok_z, tok_g,
):
    q = lax.axis_index("grp")
    lane = lax.axis_index("lane")
    zs = lanes // CORES
    core = lax.rem(lane, CORES)
    z = lane // CORES
    me = q * lanes + lane
    last = groups * lanes - 1
    rows = nblk * bs
    halo = 2 * bs
    width = ctrl_v.shape[1]

    loads = [
        pltpu.make_async_copy(ctrl_hbm, ctrl_v.at[pl.ds(halo, rows)], load_sem.at[0]),
        pltpu.make_async_copy(mass_hbm, mass_v, load_sem.at[1]),
        pltpu.make_async_copy(obs_hbm, obs_v, load_sem.at[2]),
        pltpu.make_async_copy(cols_hbm, cols_ref, load_sem.at[3]),
    ]
    def place(index):
        return (index // lanes, lax.rem(index, lanes))

    def grp_peer(k):
        return (lax.rem(q + k, groups), lane)

    def turn(i):
        return i + (1 - lax.rem(q, 2)) * (groups - 2 * i)

    def z_peer(k):
        return (q, lax.rem(z + k, zs) * CORES + core)

    partner = (q, lane + 1 - 2 * core)
    barrier = pltpu.get_barrier_semaphore()

    @pl.when(me > 0)
    def _():
        pl.semaphore_signal(barrier, inc=1, device_id=place(me - 1), device_id_type=MESH)

    @pl.when(me < last)
    def _():
        pl.semaphore_signal(barrier, inc=1, device_id=place(me + 1), device_id_type=MESH)

    def z_next(step):
        return (q, lane + step * CORES)

    def grp_near():
        if groups != 4:
            return [grp_peer(k) for k in range(1, groups)]
        return [(q + 1 - 2 * lax.rem(q, 2), lane), (lax.rem(q + 2, groups), lane)]

    peers = 0
    if fused:
        pl.semaphore_signal(barrier, inc=1, device_id=partner, device_id_type=MESH)
        for peer in grp_near():
            pl.semaphore_signal(barrier, inc=1, device_id=peer, device_id_type=MESH)
        peers = 1 + len(grp_near())

        @pl.when(z > 0)
        def _():
            pl.semaphore_signal(barrier, inc=1, device_id=z_next(-1), device_id_type=MESH)

        @pl.when(z < zs - 1)
        def _():
            pl.semaphore_signal(barrier, inc=1, device_id=z_next(1), device_id_type=MESH)

    for load in loads:
        load.start()

    lines = 0
    if fused:
        lines = (z > 0).astype(jnp.int32) + (z < zs - 1).astype(jnp.int32)
    ends = (me > 0).astype(jnp.int32) + (me < last).astype(jnp.int32)
    pl.semaphore_wait(barrier, peers + lines + ends)

    def tell_z(step):
        @pl.when(z < zs - 1)
        def _():
            pl.semaphore_signal(
                tok_z.at[0, step], inc=1, device_id=z_next(1), device_id_type=MESH
            )

        @pl.when(z > 0)
        def _():
            pl.semaphore_signal(
                tok_z.at[1, step], inc=1, device_id=z_next(-1), device_id_type=MESH
            )

    def hear_z(step):
        @pl.when(z > 0)
        def _():
            pl.semaphore_wait(tok_z.at[0, step], 1)

        @pl.when(z < zs - 1)
        def _():
            pl.semaphore_wait(tok_z.at[1, step], 1)

    steps = zs - 2 if fused else 0

    chunk = width // CHUNKS
    chunks = [slice(h * chunk, (h + 1) * chunk) for h in range(CHUNKS)]

    def to_left(h):
        return pltpu.make_async_remote_copy(
            src_ref=ctrl_v.at[pl.ds(halo, halo), chunks[h]],
            dst_ref=ctrl_v.at[pl.ds(halo + rows, halo), chunks[h]],
            send_sem=hs_sem.at[0, h],
            recv_sem=hr_sem.at[1, h],
            device_id=place(me - 1),
            device_id_type=MESH,
        )

    def to_right(h):
        return pltpu.make_async_remote_copy(
            src_ref=ctrl_v.at[pl.ds(rows, halo), chunks[h]],
            dst_ref=ctrl_v.at[pl.ds(0, halo), chunks[h]],
            send_sem=hs_sem.at[1, h],
            recv_sem=hr_sem.at[0, h],
            device_id=place(me + 1),
            device_id_type=MESH,
        )

    loads[0].wait()

    for h in range(CHUNKS):
        @pl.when(me > 0)
        def _():
            to_left(h).start()

        @pl.when(me < last)
        def _():
            to_right(h).start()

    if fused:
        if steps > 0:
            tell_z(0)
        if groups == 4:
            pl.semaphore_signal(tok_g, inc=1, device_id=grp_near()[0], device_id_type=MESH)

    @pl.when(me == 0)
    def _():
        ctrl_v[pl.ds(0, halo), :] = jnp.zeros((halo, width), BF16)

    @pl.when(me == last)
    def _():
        ctrl_v[pl.ds(halo + rows, halo), :] = jnp.zeros((halo, width), BF16)

    pairs = nblk // 2
    zero = jnp.zeros((bs, bs), BF16)
    slots = mass_v.shape[1]

    def build(p):
        for j in range(2):
            g = 2 * p + j
            offsets = []
            for s in range(1, slots):
                col = cols_ref[s, g]
                offsets.append(jnp.where(col >= 0, col - (me * nblk + g), 99))
            for b in range(6):
                d = b - 2 - j
                if d == 0:
                    block = mass_v[g, 0]
                elif abs(d) > 2:
                    block = zero
                else:
                    block = zero
                    for s in range(1, slots):
                        block = jnp.where(offsets[s - 1] == d, mass_v[g, s], block)
                band[p, j * bs:(j + 1) * bs, b * bs:(b + 1) * bs] = block

    def product(p):
        return jnp.dot(
            band[p], ctrl_v[pl.ds(pl.multiple_of(p * halo, halo), 3 * halo), :],
            preferred_element_type=F32,
        ).astype(BF16)

    order = row_order(width, lanes, fused)

    def turned(p, target, at):
        block = obs_v[pl.ds(pl.multiple_of(p * halo, halo), halo), :].T
        for source, dest, count in order:
            target[dest:dest + count, at:at + halo] = block[source:source + count, :]

    outer = core * (pairs - 1)
    inner = (1 - core) * (pairs - 1)
    inside = pl.multiple_of((1 - core) * halo, halo)
    beyond = pl.multiple_of(core * 2 * halo, halo)
    outer_row = pl.multiple_of(outer * halo, halo)

    loads[1].wait()
    loads[3].wait()
    for p in range(1, pairs - 1):
        build(p)
        mc_in[(p - 1) * halo:p * halo, :] = product(p)
    build(0)
    build(pairs - 1)
    mc_local[...] = jnp.dot(
        band[outer, :, pl.ds(inside, 2 * halo)],
        ctrl_v[pl.ds(outer_row + inside, 2 * halo), :],
        preferred_element_type=F32,
    )
    loads[2].wait()
    for p in range(1, pairs - 1):
        turned(p, obs_in, (p - 1) * halo)
    turned(inner, obs_in, (pairs - 2) * halo)
    turned(outer, obs_edge, 0)
    for step in range(steps - 1):
        hear_z(step)
        tell_z(step + 1)

    @pl.when(core == 0)
    def _():
        for h in range(CHUNKS):
            to_left(h).wait_recv()

    @pl.when(core == 1)
    def _():
        for h in range(CHUNKS):
            to_right(h).wait_recv()

    mc_in[(pairs - 2) * halo:(pairs - 1) * halo, :] = product(inner)
    half = width // 2
    for r in range(2):
        gram[r * half:(r + 1) * half, :] = jnp.dot(
            obs_in[r * half:(r + 1) * half, :], mc_in[...], preferred_element_type=F32
        )

    def edges(h):
        @pl.when((me > 0) & (core == 0))
        def _():
            to_right(h).wait_recv()

        @pl.when((me < last) & (core == 1))
        def _():
            to_left(h).wait_recv()

        mc_edge[:, chunks[h]] = (
            mc_local[:, chunks[h]]
            + jnp.dot(
                band[outer, :, pl.ds(beyond, halo)],
                ctrl_v[pl.ds(outer_row + beyond, halo), chunks[h]],
                preferred_element_type=F32,
            )
        ).astype(BF16)

    def finished(start, count, cols):
        return gram[pl.ds(start, count), cols] + jnp.dot(
            obs_edge[pl.ds(start, count), :], mc_edge[:, cols], preferred_element_type=F32
        )

    def halo_sent():
        for h in range(CHUNKS):
            @pl.when(me > 0)
            def _():
                to_left(h).wait_send()

            @pl.when(me < last)
            def _():
                to_right(h).wait_send()

    if not fused:
        for h in range(CHUNKS):
            edges(h)
        out_ref[...] = finished(0, width, slice(0, width))
        halo_sent()
        return

    theirs = pl.multiple_of((1 - core) * half, half)
    mine = pl.multiple_of(core * half, half)
    piece = width // lanes

    def copy_a(h):
        return pltpu.make_async_remote_copy(
            src_ref=send_a.at[h], dst_ref=recv_a.at[h],
            send_sem=as_sem.at[h], recv_sem=ar_sem.at[h],
            device_id=partner, device_id_type=MESH,
        )

    def copy_z(h, k):
        return pltpu.make_async_remote_copy(
            src_ref=send_z.at[h, lax.rem(z + k, zs)], dst_ref=recv_z.at[h, k - 1],
            send_sem=zs_sem.at[h, k - 1], recv_sem=zr_sem.at[h, k - 1],
            device_id=z_peer(k), device_id_type=MESH,
        )

    def copy_g(h, k):
        return pltpu.make_async_remote_copy(
            src_ref=gath.at[h, q], dst_ref=gath.at[h, q],
            send_sem=gs_sem.at[h, k - 1], recv_sem=gr_sem.at[h, k - 1],
            device_id=grp_peer(k), device_id_type=MESH,
        )

    def stage_edges(h):
        edges(h)
        send_a[h] = finished(theirs, half, chunks[h])
        copy_a(h).start()
        gram[pl.ds(mine, half), chunks[h]] = finished(mine, half, chunks[h])

    def stage_core(h):
        copy_a(h).wait_recv()
        if h == 0 and steps > 0:
            hear_z(steps - 1)
        total = gram[pl.ds(mine, half), chunks[h]] + recv_a[h]
        gram[pl.ds(mine, half), chunks[h]] = total
        send_z[h] = total.astype(BF16).reshape(zs, piece, chunk)
        for k in range(1, zs):
            copy_z(h, k).start()

    def stage_z(h):
        share = gram[pl.ds(pl.multiple_of(core * half + z * piece, piece), piece), chunks[h]]
        for k in range(1, zs):
            copy_z(h, k).wait_recv()
            share = share + recv_z[h, k - 1].astype(F32)
        gath[h, q] = share.astype(BF16)
        for i in range(1, groups):
            copy_g(h, turn(i)).start()

    def stage_grp(h):
        for k in range(1, groups):
            copy_g(h, k).wait_recv()
        total = gath[h, 0].astype(F32)
        for k in range(1, groups):
            total = total + gath[h, k].astype(F32)
        out_ref[:, chunks[h]] = total

    if groups == 4:
        pl.semaphore_wait(tok_g, 1)
    for h in range(CHUNKS):
        stage_edges(h)
        if h >= 1:
            stage_core(h - 1)
    stage_core(CHUNKS - 1)
    for h in range(CHUNKS):
        stage_z(h)
    for h in range(CHUNKS):
        stage_grp(h)
    halo_sent()
    for h in range(CHUNKS):
        copy_a(h).wait_send()
        for k in range(1, zs):
            copy_z(h, k).wait_send()
        for k in range(1, groups):
            copy_g(h, k).wait_send()


def solution(mesh):
    groups, lanes = mesh.shape["grp"], mesh.shape["lane"]

    def shards(ctrl_factor, obs_factor, block_cols, mass_blocks):
        nblk, slots = block_cols.shape
        rows, width = ctrl_factor.shape
        bs = rows // nblk
        halo = 2 * bs
        fused = width % (lanes * groups * 16) == 0
        pairs = nblk // 2
        zs = lanes // CORES
        half, chunk = width // 2, width // CHUNKS
        piece = width // lanes
        out_rows = width // lanes if fused else width
        dma = pltpu.SemaphoreType.DMA
        result = pl.pallas_call(
            functools.partial(kernel, groups, lanes, fused, nblk, bs),
            out_shape=pltpu.VMEM((out_rows, width), F32),
            in_specs=[pl.BlockSpec(memory_space=pltpu.HBM)] * 4,
            out_specs=pl.BlockSpec(memory_space=pltpu.VMEM),
            scratch_shapes=[
                pltpu.SMEM((slots, nblk), jnp.int32),
                pltpu.VMEM((rows + 2 * halo, width), BF16),
                pltpu.VMEM((rows, width), BF16),
                pltpu.VMEM((nblk, slots, bs, bs), BF16),
                pltpu.VMEM((pairs, halo, 3 * halo), BF16),
                pltpu.VMEM((width, rows - halo), BF16),
                pltpu.VMEM((width, halo), BF16),
                pltpu.VMEM((rows - halo, width), BF16),
                pltpu.VMEM((halo, width), F32),
                pltpu.VMEM((halo, width), BF16),
                pltpu.VMEM((width, width), F32),
                pltpu.VMEM((CHUNKS, half, chunk), F32),
                pltpu.VMEM((CHUNKS, half, chunk), F32),
                pltpu.VMEM((CHUNKS, zs, piece, chunk), BF16),
                pltpu.VMEM((CHUNKS, zs - 1, piece, chunk), BF16),
                pltpu.VMEM((CHUNKS, groups, piece, chunk), BF16),
                dma((4,)), dma((2, CHUNKS)), dma((2, CHUNKS)), dma((CHUNKS,)), dma((CHUNKS,)),
                dma((CHUNKS, zs - 1)), dma((CHUNKS, zs - 1)),
                dma((CHUNKS, groups - 1)), dma((CHUNKS, groups - 1)),
                pltpu.SemaphoreType.REGULAR((2, max(zs - 2, 1))), pltpu.SemaphoreType.REGULAR,
            ],
            compiler_params=pltpu.CompilerParams(
                collective_id=0, has_side_effects=True, vmem_limit_bytes=56 * 2**20
            ),
        )(block_cols.T, ctrl_factor, obs_factor, mass_blocks)
        if fused:
            return result
        share = lax.psum_scatter(result, "lane", scatter_dimension=0, tiled=True)
        return lax.psum(share, "grp")

    placed = (
        P(("grp", "lane"), None),
        P(("grp", "lane"), None),
        P(("grp", "lane"), None),
        P(("grp", "lane"), None, None, None),
    )
    return jax.shard_map(
        shards, mesh=mesh, in_specs=placed, out_specs=P("lane", None), check_vma=False
    )
```
